512 devices in a mesh: blk: 32 (over y, z_lo), group: 16 (over z_hi, x, core).
Axes of the slice: x: 4, y: 8, z: 8 (z_hi: 2, z_lo: 4; z = z_hi * 4 + z_lo), core: 2. Of those that a mesh axis runs over, the one named last changes fastest.
Arguments:
- vertex_matrix: bfloat16 [512, 1152, 1152], P(('blk', 'group')), may hold values from -0.1875 to 0.1875
- vertex_site: int32 [512, 1152], P(('blk', 'group')), may hold values from 0 to 15
- vertex_time: int32 [512, 1152], P(('blk', 'group')), may hold values from 0 to 1023
- vertex_spin: int32 [512, 1152], P(('blk', 'group')), may hold values from 0 to 1
- free_green: float32 [2, 128], replicated, may hold values from -3 to 3
- plus_table: int32 [128, 128], replicated, may hold values from 0 to 127, each once within a row
- cross_table: int32 [128, 128], P('blk'), may hold values from 0 to 127, each once within a row
Outputs:
- crossed: float32 [2, 128, 128, 128], P(None, 'blk', None, 'group')
The draws below stay inside these ranges and needn't reach their ends.
Inputs may be any that keep to these rules, and one draw needn't show every extreme that they name: `plus_table`: each row is a permutation of 0 to 127. `cross_table`: each row is a permutation of 0 to 127.
All inputs are finite; a program needn't handle non-finite values.
Results may differ from the reference program's by a relative error of at most 0.0078.
Values may be sent and summed in bfloat16 or wider, within the bound.
No kernel may reach another device: no remote copies, remote signals or barrier semaphores. Data moves between devices by JAX's collectives and lax.ppermute only.
A program may use at most 64 MiB of HBM per device.

```python
import math
import jax
import jax.numpy as jnp
from jax import lax

LX = 4
NK = 16
NW = 8
W = 128
NV = 1152
NT = 1024
NQ = 128
WALKERS = 512


def place_ends(result, own_key, low, largest):
    longest = result.shape.index(max(result.shape))
    spots = []
    for shift in (0, 1):
        where = [jax.random.randint(jax.random.fold_in(own_key, axis), (), 0, length) for axis, length in enumerate(result.shape)]
        where[longest] = (where[longest] + shift) % result.shape[longest]
        spots.append(tuple(where))
    return result.at[spots[0]].set(low).at[spots[1]].set(largest)


def shard_levels(own_key, dims, pieces, smallest, high):
    factor_of = 1.0
    for dim, shards_of in pieces:
        steps = jax.random.uniform(jax.random.fold_in(jax.random.fold_in(own_key, 6), dim), (shards_of,), jnp.float32, smallest / len(pieces), high / len(pieces))
        factor_of = factor_of * jnp.repeat(jnp.exp(steps), dims[dim] // shards_of).reshape((-1,) + (1,) * (len(dims) - 1 - dim))
    return factor_of


def noise(key, shape, deviation, most, shards=(), kind=jnp.bfloat16):
    entries = jax.random.normal(key, shape, jnp.float32) * deviation
    if len(shards) > 0:
        entries = shard_levels(key, shape, shards, -0.22, 0.18) * entries
    return jnp.clip(entries, min=-most, max=most).astype(kind)


def setup_inputs(seed: int = 0) -> dict:
    seeds = jax.random.split(jax.random.key(seed), 8)
    return {
        "vertex_matrix": noise(seeds[0], (WALKERS, NV, NV), NV ** -0.5, 0.1875, ((0, 512),)),
        "vertex_site": place_ends(jax.random.randint(seeds[1], (WALKERS, NV), 0, NK), jax.random.fold_in(seeds[1], 1), 0, NK - 1).astype(jnp.int32),
        "vertex_time": place_ends(jax.random.randint(seeds[2], (WALKERS, NV), 0, NT), jax.random.fold_in(seeds[2], 1), 0, NT - 1).astype(jnp.int32),
        "vertex_spin": place_ends(jax.random.randint(seeds[3], (WALKERS, NV), 0, 2), jax.random.fold_in(seeds[3], 1), 0, 1).astype(jnp.int32),
        "free_green": noise(seeds[4], (2, W), 0.5, 3.0, (), jnp.float32),
        "plus_table": jax.vmap(lambda own: jax.random.permutation(own, W))(jax.random.split(seeds[5], NQ)).reshape((NQ, W)).astype(jnp.int32),
        "cross_table": jax.vmap(lambda own: jax.random.permutation(own, NQ))(jax.random.split(seeds[6], W)).reshape((W, NQ)).astype(jnp.int32),
    }


def phases(site_ids, time_ids):
    points = jnp.arange(W, dtype=jnp.int32)
    moment = points // NW
    freq_index = points % NW
    kx_part = moment % LX
    ky_part = moment // LX
    rx_part = site_ids % LX
    ry_part = site_ids // LX
    winding = (2 * freq_index + 1)[:, None] * time_ids[None, :] + 2 * NT // LX * (kx_part[:, None] * rx_part[None, :] + ky_part[:, None] * ry_part[None, :])
    winding = winding % (2 * NT)
    return winding.astype(jnp.float32) * (math.pi / NT)

def green_pair(matrix, site_ids, time_ids, spin_ids, free_green):
    angles = phases(site_ids, time_ids)
    cosine = jnp.cos(angles)
    sine_part = jnp.sin(angles)
    spin_up = (spin_ids == 0).astype(jnp.float32)[None, :]
    spin_down = (spin_ids == 1).astype(jnp.float32)[None, :]
    fourier_rows = jnp.concatenate([cosine * spin_up, sine_part * spin_up, cosine * spin_down, sine_part * spin_down], 0).astype(jnp.bfloat16)
    projected = jnp.dot(fourier_rows, matrix, preferred_element_type=jnp.float32).astype(jnp.bfloat16)
    norm_factor = 1.0 / math.sqrt(NV)
    real_free = free_green[0]
    imag_free = free_green[1]
    greens = []
    for spin_index in range(2):
        offset = 2 * W * spin_index
        cosine_rows = fourier_rows[offset:offset + W]
        sine_rows = fourier_rows[offset + W:offset + 2 * W]
        proj_real = projected[offset:offset + W]
        proj_imag = projected[offset + W:offset + 2 * W]
        left_block = jnp.concatenate([jnp.concatenate([proj_real, proj_imag], 1), jnp.concatenate([proj_imag, -proj_real], 1)], 0)
        right_block = jnp.concatenate([cosine_rows, sine_rows], 1)
        kernel = lax.dot_general(left_block, right_block, (((1,), (1,)), ((), ())), preferred_element_type=jnp.float32)
        kernel_real = kernel[:W]
        kernel_imag = kernel[W:]
        half_real = real_free[:, None] * kernel_real - imag_free[:, None] * kernel_imag
        half_imag = real_free[:, None] * kernel_imag + imag_free[:, None] * kernel_real
        green_real = -(half_real * real_free[None, :] - half_imag * imag_free[None, :]) * norm_factor
        green_imag = -(half_real * imag_free[None, :] + half_imag * real_free[None, :]) * norm_factor
        greens.append(jnp.stack([green_real, green_imag], 0))
    green_sum = (greens[0] + greens[1]).astype(jnp.bfloat16)
    return (green_sum, greens[0].astype(jnp.bfloat16), greens[1].astype(jnp.bfloat16))

def pair_terms(green_sum, green_up, green_down, perm_rows):
    summed = green_sum.astype(jnp.float32)
    partner = jnp.swapaxes(summed[:, perm_rows[:, :, None], perm_rows[:, None, :]], 2, 3)
    direct_real = summed[0][None] * partner[0] - summed[1][None] * partner[1]
    direct_imag = summed[0][None] * partner[1] + summed[1][None] * partner[0]
    column_ids = jnp.arange(W, dtype=jnp.int32)[None, :]
    cross_real = jnp.zeros_like(direct_real)
    cross_imag = jnp.zeros_like(direct_imag)
    for spin_green in (green_up, green_down):
        values = spin_green.astype(jnp.float32)
        lead_values = values[:, column_ids, perm_rows]
        trail_values = values[:, perm_rows, column_ids]
        cross_real = cross_real + lead_values[0][:, :, None] * trail_values[0][:, None, :] - lead_values[1][:, :, None] * trail_values[1][:, None, :]
        cross_imag = cross_imag + lead_values[0][:, :, None] * trail_values[1][:, None, :] + lead_values[1][:, :, None] * trail_values[0][:, None, :]
    return jnp.stack([direct_real - cross_real, direct_imag - cross_imag], 0)

def reference(vertex_matrix, vertex_site, vertex_time, vertex_spin, free_green, plus_table, cross_table):

    def accumulate(running, walker):
        matrix, site_ids, time_ids, spin_ids = walker
        green_sum, green_up, green_down = green_pair(matrix, site_ids, time_ids, spin_ids, free_green)
        return (running + pair_terms(green_sum, green_up, green_down, plus_table), None)
    zero_total = jnp.zeros((2, NQ, W, W), jnp.float32)
    transfer, ignored = lax.scan(accumulate, zero_total, (vertex_matrix, vertex_site, vertex_time, vertex_spin))
    row_ids = jnp.arange(W, dtype=jnp.int32)
    return transfer[:, cross_table, row_ids[:, None], :]
```

```python
import functools
import math

import jax
import jax.numpy as jnp
from jax import lax
from jax.experimental import pallas as pl
from jax.experimental.pallas import tpu as pltpu
from jax.sharding import Mesh, PartitionSpec as P

LX = 4
NK = 16
NW = 8
W = 128
NV = 1152
NT = 1024
BROWS = 8
NEAR = 8
VMEM = pl.BlockSpec(memory_space=pltpu.VMEM)
SMEM = pl.BlockSpec(memory_space=pltpu.SMEM)
BF16 = jnp.bfloat16
F32 = jnp.float32


def green_kernel(m_ref, site_ref, time_ref, spin_ref, free_ref, out_ref, rows_ref):
    freq = lax.broadcasted_iota(jnp.int32, (NW, NV), 0)
    times = jnp.broadcast_to(time_ref[...], (NW, NV))
    sites = jnp.broadcast_to(site_ref[...], (NW, NV))
    spins = jnp.broadcast_to(spin_ref[...], (NW, NV))
    winding = ((2 * freq + 1) * times) & (2 * NT - 1)
    angles = winding.astype(F32) * (math.pi / NT)
    cosine, sine = jnp.cos(angles), jnp.sin(angles)
    rx, ry = sites & (LX - 1), sites >> 2
    up = (spins == 0).astype(F32)
    down = (spins == 1).astype(F32)
    blocks = [[], [], [], []]
    for k in range(NK):
        turns = ((k % LX) * rx + (k // LX) * ry) & 3
        odd = (turns & 1) == 1
        sign_c = jnp.where(((turns + 1) & 2) == 0, 1.0, -1.0)
        sign_s = jnp.where((turns & 2) == 0, 1.0, -1.0)
        ck = jnp.where(odd, sine, cosine) * sign_c
        sk = jnp.where(odd, cosine, sine) * sign_s
        for block, value in zip(blocks, (ck * up, sk * up, ck * down, sk * down)):
            block.append(value)
    for index, block in enumerate(blocks):
        rows_ref[index * W : (index + 1) * W, :] = jnp.concatenate(block, 0).astype(BF16)
    norm_factor = 1.0 / math.sqrt(NV)
    eye = lax.broadcasted_iota(jnp.int32, (W, W), 0) == lax.broadcasted_iota(jnp.int32, (W, W), 1)
    fr, fi = free_ref[0:1, :], free_ref[1:2, :]
    col_r = jnp.sum(jnp.where(eye, fr, 0.0), axis=1, keepdims=True)
    col_i = jnp.sum(jnp.where(eye, fi, 0.0), axis=1, keepdims=True)
    for s in range(2):
        rows = rows_ref[2 * W * s : 2 * W * (s + 1), :]
        projected = jnp.dot(rows, m_ref[0], preferred_element_type=F32).astype(BF16)
        pairs = lax.dot_general(
            projected, rows, (((1,), (1,)), ((), ())), preferred_element_type=F32
        )
        kr = pairs[:W, :W] + pairs[W:, W:]
        ki = pairs[W:, :W] - pairs[:W, W:]
        hr = col_r * kr - col_i * ki
        hi = col_r * ki + col_i * kr
        out_ref[2 * s] = (-(hr * fr - hi * fi) * norm_factor).astype(BF16)
        out_ref[2 * s + 1] = (-(hr * fi + hi * fr) * norm_factor).astype(BF16)


def pair_kernel(
    near_ref, own_ref, other_ref, plus_ref, out_ref,
    both_ref, pick_ref, lead_ref, trail_ref, col_ref, sums_ref, flat_ref,
):
    def plane(w, s, part):
        ref = own_ref if w < 4 else other_ref
        return ref[(w % 4) * 4 + 2 * s + part]

    near = near_ref[0]
    plus = plus_ref[...]
    plus_t = plus.astype(F32).T.astype(jnp.int32)
    lane = lax.broadcasted_iota(jnp.int32, (W, W), 1)
    slot = lax.broadcasted_iota(jnp.int32, (16, W), 0)
    point = lax.broadcasted_iota(jnp.int32, (16, W), 1)
    owned = (slot // 8) * 64 + near * 8 + slot % 8
    chosen = (point == owned).astype(BF16)
    plus_own = jnp.dot(chosen, plus_t.astype(F32).astype(BF16), preferred_element_type=F32)
    plus_own_i = plus_own.astype(jnp.int32)
    plus_col = plus_own.T.astype(jnp.int32)
    for b in range(16):
        hot = (plus_col[:, b : b + 1] == lane).astype(F32).astype(BF16)
        pick_ref[b * W : (b + 1) * W, 0:W] = hot
        pick_ref[b * W : (b + 1) * W, W : 2 * W] = hot
    for w in range(NEAR):
        for part in range(2):
            total = None
            for s in range(2):
                value = plane(w, s, part)
                both_ref[w, s * W : (s + 1) * W, part * W : (part + 1) * W] = value
                k = (w * 2 + s) * 2 + part
                lead_ref[k] = jnp.take_along_axis(value.astype(F32), plus_t, axis=1)
                columns = lax.dot_general(
                    chosen, value, (((1,), (1,)), ((), ())), preferred_element_type=F32
                )
                trail_ref[k] = jnp.take_along_axis(columns, plus_own_i, axis=1)
                total = columns if total is None else total + columns
            col_ref[w * 2 + part] = total

    def some(step, carry):
        start = pl.multiple_of(step * 4 * W, 4 * W)
        picks = pick_ref[pl.ds(start, 4 * W), :]
        for w in range(NEAR):
            moved = jnp.dot(picks, both_ref[w], preferred_element_type=F32)
            for j in range(4):
                row_r = col_ref[2 * w, pl.ds(step * 4 + j, 1), :]
                row_i = col_ref[2 * w + 1, pl.ds(step * 4 + j, 1), :]
                yr = jnp.take_along_axis(moved[j * W : (j + 1) * W, :W], plus, axis=1)
                yi = jnp.take_along_axis(moved[j * W : (j + 1) * W, W:], plus, axis=1)
                re = row_r * yr - row_i * yi
                im = row_r * yi + row_i * yr
                if w == 0:
                    sums_ref[2 * j] = re
                    sums_ref[2 * j + 1] = im
                else:
                    sums_ref[2 * j] += re
                    sums_ref[2 * j + 1] += im
        for j in range(4):
            b = step * 4 + j
            er = sums_ref[2 * j].T
            ei = sums_ref[2 * j + 1].T
            for k in range(2 * NEAR):
                lr, li = lead_ref[2 * k], lead_ref[2 * k + 1]
                tr = trail_ref[2 * k, pl.ds(b, 1), :]
                ti = trail_ref[2 * k + 1, pl.ds(b, 1), :]
                er = er - (lr * tr - li * ti)
                ei = ei - (lr * ti + li * tr)
            sums_ref[2 * j] = er
            sums_ref[2 * j + 1] = ei
            for part in range(2):
                for a4 in range(4):
                    piece = sums_ref[2 * j + part, pl.ds(a4, 32, stride=4), :]
                    first = (b // 8) * 64 + (part * 4 + a4) * 8 + b % 8
                    flat_ref[pl.ds(first, 32, stride=128), :] = piece
        return carry

    lax.fori_loop(0, 4, some, 0)
    out_ref[...] = flat_ref[...].astype(BF16)


def last_kernel(parts_ref, cross_ref, out_ref):
    def add(step, total):
        for j in range(8):
            total = total + parts_ref[step * 8 + j].astype(F32)
        return total

    total = lax.fori_loop(0, 8, add, jnp.zeros((64, W), F32))
    for part in range(2):
        for a4 in range(4):
            first = (part * 4 + a4) * 8
            index = jnp.broadcast_to(cross_ref[a4 : a4 + 1, :], (8, W))
            out_ref[part, a4] = jnp.take_along_axis(total[first : first + 8], index, axis=1)


def body(vertex_matrix, vertex_site, vertex_time, vertex_spin, free_green, plus_table, cross_table):
    limit = pltpu.CompilerParams(vmem_limit_bytes=48 << 20)
    green = pl.pallas_call(
        green_kernel,
        out_shape=jax.ShapeDtypeStruct((4, W, W), BF16),
        in_specs=[VMEM] * 5,
        out_specs=VMEM,
        scratch_shapes=[pltpu.VMEM((4 * W, NV), BF16)],
        compiler_params=limit,
        name="green",
    )(vertex_matrix, vertex_site, vertex_time, vertex_spin, free_green)
    own = lax.all_gather(green, "x", axis=0, tiled=True)
    other = lax.ppermute(own, "core", [(0, 1), (1, 0)])
    near = (lax.axis_index("x") * 2 + lax.axis_index("core")).reshape(1)
    partial = pl.pallas_call(
        pair_kernel,
        out_shape=jax.ShapeDtypeStruct((64 * 64, W), BF16),
        in_specs=[SMEM] + [VMEM] * 3,
        out_specs=VMEM,
        scratch_shapes=[
            pltpu.VMEM((NEAR, 2 * W, 2 * W), BF16),
            pltpu.VMEM((16 * W, 2 * W), BF16),
            pltpu.VMEM((4 * NEAR, W, W), F32),
            pltpu.VMEM((4 * NEAR, 16, W), F32),
            pltpu.VMEM((2 * NEAR, 16, W), F32),
            pltpu.VMEM((8, W, W), F32),
            pltpu.VMEM((64 * 64, W), F32),
        ],
        compiler_params=limit,
        name="pairs",
    )(near, own, other, plus_table)
    parts = lax.all_to_all(
        partial.reshape(64, 64, W), ("y", "z_lo", "z_hi"), 0, 0, tiled=True
    )
    crossed = pl.pallas_call(
        last_kernel,
        out_shape=jax.ShapeDtypeStruct((2, 4, BROWS, W), F32),
        in_specs=[VMEM] * 2,
        out_specs=VMEM,
        name="last",
    )(parts, cross_table)
    return jnp.swapaxes(crossed, 2, 3)


def solution(mesh):
    names = ("y", "z_lo", "z_hi", "x", "core")
    fine = Mesh(mesh.devices.reshape(8, 4, 2, 4, 2), names)
    rows = P(names)
    in_specs = (P(names, None, None), rows, rows, rows, P(), P(), P(("y", "z_lo"), None))
    out_specs = P(None, ("y", "z_lo"), None, ("z_hi", "x", "core"))
    return jax.shard_map(body, mesh=fine, in_specs=in_specs, out_specs=out_specs, check_vma=False)
```

```python
import functools
import math

import jax
import jax.numpy as jnp
from jax import lax
from jax.experimental import pallas as pl
from jax.experimental.pallas import tpu as pltpu
from jax.sharding import Mesh, PartitionSpec as P

LX = 4
NK = 16
NW = 8
W = 128
NV = 1152
NT = 1024
BROWS = 8
NEAR = 8
PIECE = 384
PITCH = W + 1
STEP = 4 * NEAR + 1
HBM = pl.BlockSpec(memory_space=pltpu.HBM)
VMEM = pl.BlockSpec(memory_space=pltpu.VMEM)
SMEM = pl.BlockSpec(memory_space=pltpu.SMEM)
BF16 = jnp.bfloat16
F32 = jnp.float32


def green_kernel(
    m_hbm, site_hbm, time_hbm, spin_hbm, free_hbm, out_ref,
    m_ref, site_ref, time_ref, spin_ref, free_ref, rows_ref, sems,
):
    small = [
        pltpu.make_async_copy(src, dst, sems.at[i])
        for i, (src, dst) in enumerate(
            ((site_hbm, site_ref), (time_hbm, time_ref), (spin_hbm, spin_ref), (free_hbm, free_ref))
        )
    ]
    large = [
        pltpu.make_async_copy(
            m_hbm.at[0, :, c * PIECE : (c + 1) * PIECE],
            m_ref.at[:, c * PIECE : (c + 1) * PIECE],
            sems.at[4 + c],
        )
        for c in range(NV // PIECE)
    ]
    for copy in small + large:
        copy.start()
    for copy in small:
        copy.wait()
    freq = lax.broadcasted_iota(jnp.int32, (NW, NV), 0)
    times = jnp.broadcast_to(time_ref[...], (NW, NV))
    sites = jnp.broadcast_to(site_ref[...], (NW, NV))
    spins = jnp.broadcast_to(spin_ref[...], (NW, NV))
    winding = ((2 * freq + 1) * times) & (2 * NT - 1)
    angles = winding.astype(F32) * (math.pi / NT)
    cosine, sine = jnp.cos(angles), jnp.sin(angles)
    rx, ry = sites & (LX - 1), sites >> 2
    up = (spins == 0).astype(F32)
    down = (spins == 1).astype(F32)
    for pair in range(NK // 2):
        blocks = [[], [], [], []]
        for k in (2 * pair, 2 * pair + 1):
            turns = ((k % LX) * rx + (k // LX) * ry) & 3
            odd = (turns & 1) == 1
            sign_c = jnp.where(((turns + 1) & 2) == 0, 1.0, -1.0)
            sign_s = jnp.where((turns & 2) == 0, 1.0, -1.0)
            ck = jnp.where(odd, sine, cosine) * sign_c
            sk = jnp.where(odd, cosine, sine) * sign_s
            for block, value in zip(blocks, (ck * up, sk * up, ck * down, sk * down)):
                block.append(value)
        for index, block in enumerate(blocks):
            first = index * W + pair * 2 * NW
            rows_ref[first : first + 2 * NW, :] = jnp.concatenate(block, 0).astype(BF16)
    norm_factor = 1.0 / math.sqrt(NV)
    eye = lax.broadcasted_iota(jnp.int32, (W, W), 0) == lax.broadcasted_iota(jnp.int32, (W, W), 1)
    fr, fi = free_ref[0:1, :], free_ref[1:2, :]
    col_r = jnp.sum(jnp.where(eye, fr, 0.0), axis=1, keepdims=True)
    col_i = jnp.sum(jnp.where(eye, fi, 0.0), axis=1, keepdims=True)
    pairs = [None, None]
    for c in range(NV // PIECE):
        large[c].wait()
        piece = m_ref[:, c * PIECE : (c + 1) * PIECE]
        for s in range(2):
            mine = slice(2 * W * s, 2 * W * (s + 1))
            projected = jnp.dot(rows_ref[mine, :], piece, preferred_element_type=F32)
            term = lax.dot_general(
                projected.astype(BF16),
                rows_ref[mine, c * PIECE : (c + 1) * PIECE],
                (((1,), (1,)), ((), ())),
                preferred_element_type=F32,
            )
            pairs[s] = term if c == 0 else pairs[s] + term
    for s in range(2):
        kr = pairs[s][:W, :W] + pairs[s][W:, W:]
        ki = pairs[s][W:, :W] - pairs[s][:W, W:]
        hr = col_r * kr - col_i * ki
        hi = col_r * ki + col_i * kr
        out_ref[2 * s] = (-(hr * fr - hi * fi) * norm_factor).astype(BF16)
        out_ref[2 * s + 1] = (-(hr * fi + hi * fr) * norm_factor).astype(BF16)


def pair_kernel(
    near_ref, own_ref, other_ref, plus_ref, out_ref,
    both_ref, pick_ref, lead_ref, trail_ref, spread_ref, col_ref, even_ref, odd_ref,
    sums_ref, turn_ref,
):
    def plane(w, s, part):
        ref = own_ref if w < 4 else other_ref
        return ref[(w % 4) * 4 + 2 * s + part]

    near = near_ref[0]
    plus_t = plus_ref[...].astype(F32).T.astype(jnp.int32)
    lane = lax.broadcasted_iota(jnp.int32, (W, W), 1)
    slot = lax.broadcasted_iota(jnp.int32, (16, W), 0)
    point = lax.broadcasted_iota(jnp.int32, (16, W), 1)
    owned = (slot // 8) * 64 + near * 8 + slot % 8
    chosen = (point == owned).astype(BF16)
    plus_own = jnp.dot(chosen, plus_t.astype(F32).astype(BF16), preferred_element_type=F32)
    plus_own_i = plus_own.astype(jnp.int32)
    plus_col = plus_own.T.astype(jnp.int32)
    for b in range(16):
        hot = (plus_col[:, b : b + 1] == lane).astype(F32).astype(BF16)
        pick_ref[b * W : (b + 1) * W, 0:W] = hot
        pick_ref[b * W : (b + 1) * W, W : 2 * W] = hot
    for w in range(NEAR):
        for part in range(2):
            total = None
            for s in range(2):
                value = plane(w, s, part)
                both_ref[w, s * W : (s + 1) * W, part * W : (part + 1) * W] = value
                k = (w * 2 + s) * 2 + part
                lead_ref[k * PITCH : k * PITCH + W, :] = jnp.take_along_axis(
                    value.astype(F32), plus_t, axis=1
                ).T
                columns = lax.dot_general(
                    chosen, value, (((1,), (1,)), ((), ())), preferred_element_type=F32
                )
                trail_ref[pl.ds(k, 16, stride=STEP), :] = jnp.take_along_axis(
                    columns, plus_own_i, axis=1
                )
                total = columns if total is None else total + columns
            col_ref[w * 2 + part] = total

    planes = 4 * NEAR
    from_k = lax.broadcasted_iota(jnp.int32, (planes, 16 * planes), 0)
    to_lane = lax.broadcasted_iota(jnp.int32, (planes, 16 * planes), 1)
    to_k = to_lane & (planes - 1)
    real = to_lane < 8 * planes
    repeat = jnp.where(
        real,
        jnp.where(from_k == to_k, jnp.where((to_k & 1) == 1, 1.0, -1.0), 0.0),
        jnp.where(from_k == (to_k ^ 1), -1.0, 0.0),
    ).astype(BF16)
    on = (
        (lax.broadcasted_iota(jnp.int32, (8, 16 * planes), 1) // planes) % 8
        == lax.broadcasted_iota(jnp.int32, (8, 16 * planes), 0)
    ).astype(F32)
    for b in range(16):
        turned = trail_ref[b * STEP : b * STEP + planes, :].T.astype(BF16)
        spread_ref[b * W : (b + 1) * W, :] = jnp.dot(
            turned, repeat, preferred_element_type=F32
        ) * jnp.tile(on, (16, 1))
    def exchange(t, carry):
        left = jnp.concatenate(
            [
                spread_ref[
                    pl.ds(pl.multiple_of(b * W + t * 8, 8), 8),
                    part * 8 * planes : (part + 1) * 8 * planes,
                ]
                for part in range(2)
                for b in range(16)
            ],
            0,
        ).astype(BF16)
        right = jnp.concatenate(
            [lead_ref[pl.ds(t * 8 + j, planes, stride=PITCH), :] for j in range(8)], 0
        ).astype(BF16)
        term = jnp.dot(left, right, preferred_element_type=F32)
        for part in range(2):
            for b in range(16):
                first = (part * 16 + b) * 8
                sums_ref[2 * b + part, pl.ds(pl.multiple_of(t * 8, 8), 8), :] = term[first : first + 8]
        return carry

    lax.fori_loop(0, 16, exchange, 0)

    def fetch(group, w, dst):
        picks = pick_ref[group * 4 * W : (group + 1) * 4 * W, :]
        dst[w] = jnp.dot(picks, both_ref[w], preferred_element_type=F32)

    buffers = (even_ref, odd_ref)
    for w in range(NEAR):
        fetch(0, w, even_ref)
    for group in range(4):
        now, later = buffers[group % 2], buffers[(group + 1) % 2]

        def direct(step, carry):
            for half in range(4):
                if group < 3 and half % 2 == 0:
                    fetch(group + 1, step * 2 + half // 2, later)
                start = pl.multiple_of(step * 32 + half * 8, 8)
                rows = pl.ds(start, 8)
                index = plus_ref[rows, :]
                for j in range(4):
                    b = group * 4 + j
                    mine = pl.ds(pl.multiple_of(j * W + start, 8), 8)
                    re, im = sums_ref[2 * b, rows, :], sums_ref[2 * b + 1, rows, :]
                    for v in range(NEAR):
                        row_r = col_ref[2 * v, pl.ds(b, 8, stride=0), :]
                        row_i = col_ref[2 * v + 1, pl.ds(b, 8, stride=0), :]
                        yr = jnp.take_along_axis(now[v, mine, 0:W], index, axis=1)
                        yi = jnp.take_along_axis(now[v, mine, W : 2 * W], index, axis=1)
                        re = re + (row_r * yr - row_i * yi)
                        im = im + (row_r * yi + row_i * yr)
                    sums_ref[2 * b, rows, :] = re
                    sums_ref[2 * b + 1, rows, :] = im
            return carry

        lax.fori_loop(0, W // 32, direct, 0)

    def turn(step, carry):
        for j in range(4):
            b = step * 4 + j
            for part in range(2):
                turn_ref[pl.ds((part * 16 + b) * PITCH, W), :] = sums_ref[2 * b + part].T
        return carry

    lax.fori_loop(0, 4, turn, 0)

    def place(step, carry):
        for near_i, high in ((0, 0), (0, 1), (1, 0), (1, 1), (2, 0), (2, 1), (3, 0), (3, 1)):
            i = step * 4 + near_i
            for part in range(2):
                for a4 in (0, 2):
                    tiles = [
                        turn_ref[pl.ds((part * 16 + high * 8) * PITCH + i * 4 + a, 8, stride=PITCH), :]
                        for a in (a4, a4 + 1)
                    ]
                    first = pl.multiple_of((i * 2 + high) * 64 + (part * 4 + a4) * 8, 16)
                    out_ref[pl.ds(first, 16), :] = jnp.concatenate(tiles, 0).astype(BF16)
        return carry

    lax.fori_loop(0, 8, place, 0)


def last_kernel(parts_ref, cross_ref, out_ref):
    def add(step, total):
        for j in range(8):
            total = total + parts_ref[step * 8 + j].astype(F32)
        return total

    total = lax.fori_loop(0, 8, add, jnp.zeros((64, W), F32))
    for part in range(2):
        for a4 in range(4):
            first = (part * 4 + a4) * 8
            index = jnp.broadcast_to(cross_ref[a4 : a4 + 1, :], (8, W))
            out_ref[part, a4] = jnp.take_along_axis(total[first : first + 8], index, axis=1)


def body(vertex_matrix, vertex_site, vertex_time, vertex_spin, free_green, plus_table, cross_table):
    limit = pltpu.CompilerParams(vmem_limit_bytes=48 << 20)
    green = pl.pallas_call(
        green_kernel,
        out_shape=jax.ShapeDtypeStruct((4, W, W), BF16),
        in_specs=[HBM] * 5,
        out_specs=VMEM,
        scratch_shapes=[
            pltpu.VMEM((NV, NV), BF16),
            pltpu.VMEM((1, NV), jnp.int32),
            pltpu.VMEM((1, NV), jnp.int32),
            pltpu.VMEM((1, NV), jnp.int32),
            pltpu.VMEM((2, W), F32),
            pltpu.VMEM((4 * W, NV), BF16),
            pltpu.SemaphoreType.DMA((4 + NV // PIECE,)),
        ],
        compiler_params=limit,
        name="green",
    )(vertex_matrix, vertex_site, vertex_time, vertex_spin, free_green)
    own = lax.all_gather(green, "x", axis=0, tiled=True)
    other = lax.ppermute(own, "core", [(0, 1), (1, 0)])
    near = (lax.axis_index("x") * 2 + lax.axis_index("core")).reshape(1)
    partial = pl.pallas_call(
        pair_kernel,
        out_shape=jax.ShapeDtypeStruct((64 * 64, W), BF16),
        in_specs=[SMEM] + [VMEM] * 3,
        out_specs=VMEM,
        scratch_shapes=[
            pltpu.VMEM((NEAR, 2 * W, 2 * W), BF16),
            pltpu.VMEM((16 * W, 2 * W), BF16),
            pltpu.VMEM((4 * NEAR * PITCH, W), F32),
            pltpu.VMEM((16 * STEP, W), F32),
            pltpu.VMEM((16 * W, 16 * 4 * NEAR), F32),
            pltpu.VMEM((2 * NEAR, 16, W), F32),
            pltpu.VMEM((NEAR, 4 * W, 2 * W), F32),
            pltpu.VMEM((NEAR, 4 * W, 2 * W), F32),
            pltpu.VMEM((32, W, W), F32),
            pltpu.VMEM((32 * PITCH, W), F32),
        ],
        compiler_params=limit,
        name="pairs",
    )(near, own, other, plus_table)
    parts = lax.all_to_all(
        partial.reshape(64, 64, W), ("y", "z_lo", "z_hi"), 0, 0, tiled=True
    )
    crossed = pl.pallas_call(
        last_kernel,
        out_shape=jax.ShapeDtypeStruct((2, 4, BROWS, W), F32),
        in_specs=[VMEM] * 2,
        out_specs=VMEM,
        name="last",
    )(parts, cross_table)
    return jnp.swapaxes(crossed, 2, 3)


def solution(mesh):
    names = ("y", "z_lo", "z_hi", "x", "core")
    fine = Mesh(mesh.devices.reshape(8, 4, 2, 4, 2), names)
    rows = P(names)
    in_specs = (P(names, None, None), rows, rows, rows, P(), P(), P(("y", "z_lo"), None))
    out_specs = P(None, ("y", "z_lo"), None, ("z_hi", "x", "core"))
    return jax.shard_map(body, mesh=fine, in_specs=in_specs, out_specs=out_specs, check_vma=False)
```

```python
import functools
import math

import jax
import jax.numpy as jnp
from jax import lax
from jax.experimental import pallas as pl
from jax.experimental.pallas import tpu as pltpu
from jax.sharding import Mesh, PartitionSpec as P

LX = 4
NK = 16
NW = 8
W = 128
NV = 1152
NT = 1024
BROWS = 8
NEAR = 8
PIECE = 384
PITCH = W + 1
STEP = 4 * NEAR + 1
ANY = pl.BlockSpec(memory_space=pl.ANY)
VMEM = pl.BlockSpec(memory_space=pltpu.VMEM)
SMEM = pl.BlockSpec(memory_space=pltpu.SMEM)
BF16 = jnp.bfloat16
F32 = jnp.float32


def green_kernel(
    m_hbm, site_hbm, time_hbm, spin_hbm, free_hbm, out_ref,
    m_ref, site_ref, time_ref, spin_ref, free_ref, rows_ref, sems,
):
    small = [
        pltpu.make_async_copy(src, dst, sems.at[i])
        for i, (src, dst) in enumerate(
            ((site_hbm, site_ref), (time_hbm, time_ref), (spin_hbm, spin_ref), (free_hbm, free_ref))
        )
    ]
    large = [
        pltpu.make_async_copy(
            m_hbm.at[0, :, c * PIECE : (c + 1) * PIECE],
            m_ref.at[:, c * PIECE : (c + 1) * PIECE],
            sems.at[4 + c],
        )
        for c in range(NV // PIECE)
    ]
    for copy in small + large:
        copy.start()
    for copy in small:
        copy.wait()
    freq = lax.broadcasted_iota(jnp.int32, (NW, NV), 0)
    times = jnp.broadcast_to(time_ref[...], (NW, NV))
    sites = jnp.broadcast_to(site_ref[...], (NW, NV))
    spins = jnp.broadcast_to(spin_ref[...], (NW, NV))
    winding = ((2 * freq + 1) * times) & (2 * NT - 1)
    angles = winding.astype(F32) * (math.pi / NT)
    cosine, sine = jnp.cos(angles), jnp.sin(angles)
    rx, ry = sites & (LX - 1), sites >> 2
    up = (spins == 0).astype(F32)
    down = (spins == 1).astype(F32)
    for pair in range(NK // 2):
        blocks = [[], [], [], []]
        for k in (2 * pair, 2 * pair + 1):
            turns = ((k % LX) * rx + (k // LX) * ry) & 3
            odd = (turns & 1) == 1
            sign_c = jnp.where(((turns + 1) & 2) == 0, 1.0, -1.0)
            sign_s = jnp.where((turns & 2) == 0, 1.0, -1.0)
            ck = jnp.where(odd, sine, cosine) * sign_c
            sk = jnp.where(odd, cosine, sine) * sign_s
            for block, value in zip(blocks, (ck * up, sk * up, ck * down, sk * down)):
                block.append(value)
        for index, block in enumerate(blocks):
            first = index * W + pair * 2 * NW
            rows_ref[first : first + 2 * NW, :] = jnp.concatenate(block, 0).astype(BF16)
    norm_factor = 1.0 / math.sqrt(NV)
    eye = lax.broadcasted_iota(jnp.int32, (W, W), 0) == lax.broadcasted_iota(jnp.int32, (W, W), 1)
    fr, fi = free_ref[0:1, :], free_ref[1:2, :]
    col_r = jnp.sum(jnp.where(eye, fr, 0.0), axis=1, keepdims=True)
    col_i = jnp.sum(jnp.where(eye, fi, 0.0), axis=1, keepdims=True)
    pairs = [None, None]
    for c in range(NV // PIECE):
        large[c].wait()
        piece = m_ref[:, c * PIECE : (c + 1) * PIECE]
        for s in range(2):
            mine = slice(2 * W * s, 2 * W * (s + 1))
            projected = jnp.dot(rows_ref[mine, :], piece, preferred_element_type=F32)
            term = lax.dot_general(
                projected.astype(BF16),
                rows_ref[mine, c * PIECE : (c + 1) * PIECE],
                (((1,), (1,)), ((), ())),
                preferred_element_type=F32,
            )
            pairs[s] = term if c == 0 else pairs[s] + term
    for s in range(2):
        kr = pairs[s][:W, :W] + pairs[s][W:, W:]
        ki = pairs[s][W:, :W] - pairs[s][:W, W:]
        hr = col_r * kr - col_i * ki
        hi = col_r * ki + col_i * kr
        out_ref[2 * s] = (-(hr * fr - hi * fi) * norm_factor).astype(BF16)
        out_ref[2 * s + 1] = (-(hr * fi + hi * fr) * norm_factor).astype(BF16)


def pair_kernel(
    near_ref, own_ref, other_ref, plus_ref, out_ref,
    both_ref, pick_ref, lead_ref, trail_ref, spread_ref, col_ref, even_ref, odd_ref,
    sums_ref, straight_ref, turn_ref,
):
    def plane(w, s, part):
        ref = own_ref if w < 4 else other_ref
        return ref[(w % 4) * 4 + 2 * s + part]

    near = near_ref[0]
    plus_t = plus_ref[...].astype(F32).T.astype(jnp.int32)
    lane = lax.broadcasted_iota(jnp.int32, (W, W), 1)
    slot = lax.broadcasted_iota(jnp.int32, (16, W), 0)
    point = lax.broadcasted_iota(jnp.int32, (16, W), 1)
    owned = (slot // 8) * 64 + near * 8 + slot % 8
    chosen = (point == owned).astype(BF16)
    plus_own = jnp.dot(chosen, plus_t.astype(F32).astype(BF16), preferred_element_type=F32)
    plus_own_i = plus_own.astype(jnp.int32)
    plus_col = plus_own.T.astype(jnp.int32)
    for b in range(16):
        hot = (plus_col[:, b : b + 1] == lane).astype(F32).astype(BF16)
        pick_ref[b * W : (b + 1) * W, 0:W] = hot
        pick_ref[b * W : (b + 1) * W, W : 2 * W] = hot
    eye = (lax.broadcasted_iota(jnp.int32, (W, W), 0) == lane).astype(F32).astype(BF16)

    def fetch(group, w, dst):
        picks = pick_ref[group * 4 * W : (group + 1) * 4 * W, :]
        dst[w] = jnp.dot(picks, both_ref[w], preferred_element_type=F32)

    for w in range(NEAR):
        for part in range(2):
            total = None
            for s in range(2):
                value = plane(w, s, part)
                both_ref[w, s * W : (s + 1) * W, part * W : (part + 1) * W] = value
                k = (w * 2 + s) * 2 + part
                lead = jnp.take_along_axis(value.astype(F32), plus_t, axis=1).astype(BF16)
                lead_ref[k * PITCH : k * PITCH + W, :] = lax.dot_general(
                    eye, lead, (((1,), (1,)), ((), ())), preferred_element_type=F32
                )
                columns = lax.dot_general(
                    chosen, value, (((1,), (1,)), ((), ())), preferred_element_type=F32
                )
                trail_ref[pl.ds(k, 16, stride=STEP), :] = jnp.take_along_axis(
                    columns, plus_own_i, axis=1
                )
                total = columns if total is None else total + columns
            col_ref[w * 2 + part] = total
        fetch(0, w, even_ref)

    planes = 4 * NEAR
    from_k = lax.broadcasted_iota(jnp.int32, (planes, 16 * planes), 0)
    to_lane = lax.broadcasted_iota(jnp.int32, (planes, 16 * planes), 1)
    to_k = to_lane & (planes - 1)
    real = to_lane < 8 * planes
    repeat = jnp.where(
        real,
        jnp.where(from_k == to_k, jnp.where((to_k & 1) == 1, 1.0, -1.0), 0.0),
        jnp.where(from_k == (to_k ^ 1), -1.0, 0.0),
    ).astype(BF16)
    on = (
        (lax.broadcasted_iota(jnp.int32, (8, 16 * planes), 1) // planes) % 8
        == lax.broadcasted_iota(jnp.int32, (8, 16 * planes), 0)
    ).astype(F32)
    for b in range(16):
        turned = trail_ref[b * STEP : b * STEP + planes, :].T.astype(BF16)
        spread_ref[b * W : (b + 1) * W, :] = jnp.dot(
            turned, repeat, preferred_element_type=F32
        ) * jnp.tile(on, (16, 1))

    def exchange(t):
        left = jnp.concatenate(
            [
                spread_ref[
                    pl.ds(pl.multiple_of(b * W + t * 8, 8), 8),
                    part * 8 * planes : (part + 1) * 8 * planes,
                ]
                for part in range(2)
                for b in range(16)
            ],
            0,
        ).astype(BF16)
        right = jnp.concatenate(
            [lead_ref[pl.ds(t * 8 + j, planes, stride=PITCH), :] for j in range(8)], 0
        ).astype(BF16)
        term = jnp.dot(left, right, preferred_element_type=F32)
        for part in range(2):
            for b in range(16):
                first = (part * 16 + b) * 8
                sums_ref[2 * b + part, pl.ds(pl.multiple_of(t * 8, 8), 8), :] = term[first : first + 8]

    buffers = (even_ref, odd_ref)
    for group in range(4):
        now, later = buffers[group % 2], buffers[(group + 1) % 2]

        def direct(step, carry):
            for half in range(4):
                if group < 3 and half % 2 == 0:
                    fetch(group + 1, step * 2 + half // 2, later)
                start = pl.multiple_of(step * 32 + half * 8, 8)
                rows = pl.ds(start, 8)
                index = plus_ref[rows, :]
                for j in range(4):
                    b = group * 4 + j
                    mine = pl.ds(pl.multiple_of(j * W + start, 8), 8)
                    re = im = None
                    for v in range(NEAR):
                        row_r = col_ref[2 * v, pl.ds(b, 8, stride=0), :]
                        row_i = col_ref[2 * v + 1, pl.ds(b, 8, stride=0), :]
                        yr = jnp.take_along_axis(now[v, mine, 0:W], index, axis=1)
                        yi = jnp.take_along_axis(now[v, mine, W : 2 * W], index, axis=1)
                        add_r, add_i = row_r * yr - row_i * yi, row_r * yi + row_i * yr
                        re = add_r if v == 0 else re + add_r
                        im = add_i if v == 0 else im + add_i
                    straight_ref[2 * b, rows, :] = re
                    straight_ref[2 * b + 1, rows, :] = im
                if group == 0:
                    exchange(step * 4 + half)
            return carry

        lax.fori_loop(0, W // 32, direct, 0)

    def turn(step, carry):
        for j in range(4):
            b = step * 4 + j
            for part in range(2):
                turn_ref[pl.ds((part * 16 + b) * PITCH, W), :] = (straight_ref[2 * b + part] + sums_ref[2 * b + part]).T
        return carry

    lax.fori_loop(0, 4, turn, 0)

    def place(step, carry):
        for near_i, high in ((0, 0), (0, 1), (1, 0), (1, 1), (2, 0), (2, 1), (3, 0), (3, 1)):
            i = step * 4 + near_i
            for part in range(2):
                for a4 in (0, 2):
                    tiles = [
                        turn_ref[pl.ds((part * 16 + high * 8) * PITCH + i * 4 + a, 8, stride=PITCH), :]
                        for a in (a4, a4 + 1)
                    ]
                    first = pl.multiple_of((i * 2 + high) * 64 + (part * 4 + a4) * 8, 16)
                    out_ref[pl.ds(first, 16), :] = jnp.concatenate(tiles, 0).astype(BF16)
        return carry

    lax.fori_loop(0, 8, place, 0)


def last_kernel(parts_ref, cross_ref, out_ref):
    def add(step, total):
        for j in range(8):
            total = total + parts_ref[step * 8 + j].astype(F32)
        return total

    total = lax.fori_loop(0, 8, add, jnp.zeros((64, W), F32))
    for part in range(2):
        for a4 in range(4):
            first = (part * 4 + a4) * 8
            index = jnp.broadcast_to(cross_ref[a4 : a4 + 1, :], (8, W))
            out_ref[part, a4] = jnp.take_along_axis(total[first : first + 8], index, axis=1)


def body(vertex_matrix, vertex_site, vertex_time, vertex_spin, free_green, plus_table, cross_table):
    limit = pltpu.CompilerParams(vmem_limit_bytes=48 << 20)
    green = pl.pallas_call(
        green_kernel,
        out_shape=jax.ShapeDtypeStruct((4, W, W), BF16),
        in_specs=[ANY] * 5,
        out_specs=VMEM,
        scratch_shapes=[
            pltpu.VMEM((NV, NV), BF16),
            pltpu.VMEM((1, NV), jnp.int32),
            pltpu.VMEM((1, NV), jnp.int32),
            pltpu.VMEM((1, NV), jnp.int32),
            pltpu.VMEM((2, W), F32),
            pltpu.VMEM((4 * W, NV), BF16),
            pltpu.SemaphoreType.DMA((4 + NV // PIECE,)),
        ],
        compiler_params=pltpu.CompilerParams(vmem_limit_bytes=67043328),
        name="green",
    )(vertex_matrix, vertex_site, vertex_time, vertex_spin, free_green)
    own = lax.all_gather(green, "x", axis=0, tiled=True)
    other = lax.ppermute(own, "core", [(0, 1), (1, 0)])
    near = (lax.axis_index("x") * 2 + lax.axis_index("core")).reshape(1)
    partial = pl.pallas_call(
        pair_kernel,
        out_shape=jax.ShapeDtypeStruct((64 * 64, W), BF16),
        in_specs=[SMEM] + [VMEM] * 3,
        out_specs=VMEM,
        scratch_shapes=[
            pltpu.VMEM((NEAR, 2 * W, 2 * W), BF16),
            pltpu.VMEM((16 * W, 2 * W), BF16),
            pltpu.VMEM((4 * NEAR * PITCH, W), F32),
            pltpu.VMEM((16 * STEP, W), F32),
            pltpu.VMEM((16 * W, 16 * 4 * NEAR), F32),
            pltpu.VMEM((2 * NEAR, 16, W), F32),
            pltpu.VMEM((NEAR, 4 * W, 2 * W), F32),
            pltpu.VMEM((NEAR, 4 * W, 2 * W), F32),
            pltpu.VMEM((32, W, W), F32),
            pltpu.VMEM((32, W, W), F32),
            pltpu.VMEM((32 * PITCH, W), F32),
        ],
        compiler_params=limit,
        name="pairs",
    )(near, own, other, plus_table)
    parts = lax.all_to_all(
        partial.reshape(64, 64, W), ("y", "z_lo", "z_hi"), 0, 0, tiled=True
    )
    crossed = pl.pallas_call(
        last_kernel,
        out_shape=jax.ShapeDtypeStruct((2, 4, BROWS, W), F32),
        in_specs=[VMEM] * 2,
        out_specs=VMEM,
        name="last",
    )(parts, cross_table)
    return jnp.swapaxes(crossed, 2, 3)


def solution(mesh):
    names = ("y", "z_lo", "z_hi", "x", "core")
    fine = Mesh(mesh.devices.reshape(8, 4, 2, 4, 2), names)
    rows = P(names)
    in_specs = (P(names, None, None), rows, rows, rows, P(), P(), P(("y", "z_lo"), None))
    out_specs = P(None, ("y", "z_lo"), None, ("z_hi", "x", "core"))
    return jax.shard_map(body, mesh=fine, in_specs=in_specs, out_specs=out_specs, check_vma=False)
```

```python
import functools
import math

import jax
import jax.numpy as jnp
from jax import lax
from jax.experimental import pallas as pl
from jax.experimental.pallas import tpu as pltpu
from jax.sharding import Mesh, PartitionSpec as P

LX = 4
NK = 16
NW = 8
W = 128
NV = 1152
NT = 1024
BROWS = 8
NEAR = 8
PIECE = 384
PITCH = W + 1
STEP = 4 * NEAR + 1
ANY = pl.BlockSpec(memory_space=pl.ANY)
VMEM = pl.BlockSpec(memory_space=pltpu.VMEM)
SMEM = pl.BlockSpec(memory_space=pltpu.SMEM)
BF16 = jnp.bfloat16
F32 = jnp.float32


def green_kernel(
    m_hbm, site_hbm, time_hbm, spin_hbm, free_hbm, out_ref,
    m_ref, site_ref, time_ref, spin_ref, free_ref, rows_ref, sems,
):
    small = [
        pltpu.make_async_copy(src, dst, sems.at[i])
        for i, (src, dst) in enumerate(
            ((site_hbm, site_ref), (time_hbm, time_ref), (spin_hbm, spin_ref), (free_hbm, free_ref))
        )
    ]
    large = [
        pltpu.make_async_copy(
            m_hbm.at[0, :, c * PIECE : (c + 1) * PIECE],
            m_ref.at[:, c * PIECE : (c + 1) * PIECE],
            sems.at[4 + c],
        )
        for c in range(NV // PIECE)
    ]
    for copy in small + large:
        copy.start()
    for copy in small:
        copy.wait()
    freq = lax.broadcasted_iota(jnp.int32, (NW, NV), 0)
    times = jnp.broadcast_to(time_ref[...], (NW, NV))
    sites = jnp.broadcast_to(site_ref[...], (NW, NV))
    spins = jnp.broadcast_to(spin_ref[...], (NW, NV))
    winding = ((2 * freq + 1) * times) & (2 * NT - 1)
    angles = winding.astype(F32) * (math.pi / NT)
    cosine, sine = jnp.cos(angles), jnp.sin(angles)
    rx, ry = sites & (LX - 1), sites >> 2
    up = (spins == 0).astype(F32)
    down = (spins == 1).astype(F32)
    for pair in range(NK // 2):
        blocks = [[], [], [], []]
        for k in (2 * pair, 2 * pair + 1):
            turns = ((k % LX) * rx + (k // LX) * ry) & 3
            odd = (turns & 1) == 1
            sign_c = jnp.where(((turns + 1) & 2) == 0, 1.0, -1.0)
            sign_s = jnp.where((turns & 2) == 0, 1.0, -1.0)
            ck = jnp.where(odd, sine, cosine) * sign_c
            sk = jnp.where(odd, cosine, sine) * sign_s
            for block, value in zip(blocks, (ck * up, sk * up, ck * down, sk * down)):
                block.append(value)
        for index, block in enumerate(blocks):
            first = index * W + pair * 2 * NW
            rows_ref[first : first + 2 * NW, :] = jnp.concatenate(block, 0).astype(BF16)
    norm_factor = 1.0 / math.sqrt(NV)
    eye = lax.broadcasted_iota(jnp.int32, (W, W), 0) == lax.broadcasted_iota(jnp.int32, (W, W), 1)
    fr, fi = free_ref[0:1, :], free_ref[1:2, :]
    col_r = jnp.sum(jnp.where(eye, fr, 0.0), axis=1, keepdims=True)
    col_i = jnp.sum(jnp.where(eye, fi, 0.0), axis=1, keepdims=True)
    pairs = [None, None]
    for c in range(NV // PIECE):
        large[c].wait()
        piece = m_ref[:, c * PIECE : (c + 1) * PIECE]
        for s in range(2):
            mine = slice(2 * W * s, 2 * W * (s + 1))
            projected = jnp.dot(rows_ref[mine, :], piece, preferred_element_type=F32)
            term = lax.dot_general(
                projected.astype(BF16),
                rows_ref[mine, c * PIECE : (c + 1) * PIECE],
                (((1,), (1,)), ((), ())),
                preferred_element_type=F32,
            )
            pairs[s] = term if c == 0 else pairs[s] + term
    for s in range(2):
        kr = pairs[s][:W, :W] + pairs[s][W:, W:]
        ki = pairs[s][W:, :W] - pairs[s][:W, W:]
        hr = col_r * kr - col_i * ki
        hi = col_r * ki + col_i * kr
        out_ref[2 * s] = (-(hr * fr - hi * fi) * norm_factor).astype(BF16)
        out_ref[2 * s + 1] = (-(hr * fi + hi * fr) * norm_factor).astype(BF16)


def pair_kernel(
    near_ref, own_ref, other_ref, plus_ref, out_ref,
    both_ref, pick_ref, lead_ref, trail_ref, spread_ref, col_ref, even_ref, odd_ref,
    sums_ref, straight_ref, turn_ref,
):
    def plane(w, s, part):
        ref = own_ref if w < 4 else other_ref
        return ref[(w % 4) * 4 + 2 * s + part]

    near = near_ref[0]
    plus_t = plus_ref[...].astype(F32).T.astype(jnp.int32)
    lane = lax.broadcasted_iota(jnp.int32, (W, W), 1)
    slot = lax.broadcasted_iota(jnp.int32, (16, W), 0)
    point = lax.broadcasted_iota(jnp.int32, (16, W), 1)
    owned = (slot // 8) * 64 + near * 8 + slot % 8
    chosen = (point == owned).astype(BF16)
    plus_own = jnp.dot(chosen, plus_t.astype(F32).astype(BF16), preferred_element_type=F32)
    plus_own_i = plus_own.astype(jnp.int32)
    plus_col = plus_own.T.astype(jnp.int32)
    for b in range(16):
        hot = (plus_col[:, b : b + 1] == lane).astype(F32).astype(BF16)
        pick_ref[b * W : (b + 1) * W, 0:W] = hot
        pick_ref[b * W : (b + 1) * W, W : 2 * W] = hot
    eye = (lax.broadcasted_iota(jnp.int32, (W, W), 0) == lane).astype(F32).astype(BF16)

    def fetch(group, w, dst):
        picks = pick_ref[group * 4 * W : (group + 1) * 4 * W, :]
        dst[w] = jnp.dot(picks, both_ref[w], preferred_element_type=F32)

    for w in range(NEAR):
        for part in range(2):
            total = None
            for s in range(2):
                value = plane(w, s, part)
                both_ref[w, s * W : (s + 1) * W, part * W : (part + 1) * W] = value
                k = (w * 2 + s) * 2 + part
                lead = jnp.take_along_axis(value.astype(F32), plus_t, axis=1).astype(BF16)
                lead_ref[k * PITCH : k * PITCH + W, :] = lax.dot_general(
                    eye, lead, (((1,), (1,)), ((), ())), preferred_element_type=F32
                )
                columns = lax.dot_general(
                    chosen, value, (((1,), (1,)), ((), ())), preferred_element_type=F32
                )
                trail_ref[pl.ds(k, 16, stride=STEP), :] = jnp.take_along_axis(
                    columns, plus_own_i, axis=1
                )
                total = columns if total is None else total + columns
            col_ref[w * 2 + part] = total
        fetch(0, w, even_ref)

    planes = 4 * NEAR
    from_k = lax.broadcasted_iota(jnp.int32, (planes, 16 * planes), 0)
    to_lane = lax.broadcasted_iota(jnp.int32, (planes, 16 * planes), 1)
    to_k = to_lane & (planes - 1)
    real = to_lane < 8 * planes
    repeat = jnp.where(
        real,
        jnp.where(from_k == to_k, jnp.where((to_k & 1) == 1, 1.0, -1.0), 0.0),
        jnp.where(from_k == (to_k ^ 1), -1.0, 0.0),
    ).astype(BF16)
    on = (
        (lax.broadcasted_iota(jnp.int32, (8, 16 * planes), 1) // planes) % 8
        == lax.broadcasted_iota(jnp.int32, (8, 16 * planes), 0)
    ).astype(F32)
    for b in range(16):
        turned = trail_ref[b * STEP : b * STEP + planes, :].T.astype(BF16)
        spread_ref[b * W : (b + 1) * W, :] = jnp.dot(
            turned, repeat, preferred_element_type=F32
        ) * jnp.tile(on, (16, 1))

    def exchange(t):
        left = jnp.concatenate(
            [
                spread_ref[
                    pl.ds(pl.multiple_of(b * W + t * 8, 8), 8),
                    part * 8 * planes : (part + 1) * 8 * planes,
                ]
                for part in range(2)
                for b in range(16)
            ],
            0,
        ).astype(BF16)
        right = jnp.concatenate(
            [lead_ref[pl.ds(t * 8 + j, planes, stride=PITCH), :] for j in range(8)], 0
        ).astype(BF16)
        term = jnp.dot(left, right, preferred_element_type=F32)
        for part in range(2):
            for b in range(16):
                first = (part * 16 + b) * 8
                sums_ref[2 * b + part, pl.ds(pl.multiple_of(t * 8, 8), 8), :] = term[first : first + 8]

    buffers = (even_ref, odd_ref)
    for group in range(4):
        now, later = buffers[group % 2], buffers[(group + 1) % 2]

        def direct(step, carry):
            for half in range(4):
                if group < 3 and half % 2 == 0:
                    fetch(group + 1, step * 2 + half // 2, later)
                start = pl.multiple_of(step * 32 + half * 8, 8)
                rows = pl.ds(start, 8)
                index = plus_ref[rows, :]
                for j in range(4):
                    b = group * 4 + j
                    mine = pl.ds(pl.multiple_of(j * W + start, 8), 8)
                    re = im = None
                    for v in range(NEAR):
                        row_r = col_ref[2 * v, pl.ds(b, 8, stride=0), :]
                        row_i = col_ref[2 * v + 1, pl.ds(b, 8, stride=0), :]
                        yr = jnp.take_along_axis(now[v, mine, 0:W], index, axis=1)
                        yi = jnp.take_along_axis(now[v, mine, W : 2 * W], index, axis=1)
                        add_r, add_i = row_r * yr - row_i * yi, row_r * yi + row_i * yr
                        re = add_r if v == 0 else re + add_r
                        im = add_i if v == 0 else im + add_i
                    straight_ref[2 * b, rows, :] = re
                    straight_ref[2 * b + 1, rows, :] = im
                if group == 0:
                    exchange(step * 4 + half)
            return carry

        lax.fori_loop(0, W // 32, direct, 0)

    def turn(step, carry):
        for j in range(4):
            b = step * 4 + j
            for part in range(2):
                turn_ref[pl.ds((part * 16 + b) * PITCH, W), :] = (straight_ref[2 * b + part] + sums_ref[2 * b + part]).T
        return carry

    lax.fori_loop(0, 4, turn, 0)

    def place(step, carry):
        for near_i, high in ((0, 0), (0, 1), (1, 0), (1, 1), (2, 0), (2, 1), (3, 0), (3, 1)):
            i = step * 4 + near_i
            for part in range(2):
                for a4 in (0, 2):
                    tiles = [
                        turn_ref[pl.ds((part * 16 + high * 8) * PITCH + i * 4 + a, 8, stride=PITCH), :]
                        for a in (a4, a4 + 1)
                    ]
                    first = pl.multiple_of((i * 2 + high) * 64 + (part * 4 + a4) * 8, 16)
                    out_ref[pl.ds(first, 16), :] = jnp.concatenate(tiles, 0).astype(BF16)
        return carry

    lax.fori_loop(0, 8, place, 0)


def last_kernel(parts_ref, cross_ref, out_ref):
    def add(step, total):
        for j in range(8):
            total = total + parts_ref[step * 8 + j].astype(F32)
        return total

    total = lax.fori_loop(0, 8, add, jnp.zeros((64, W), F32))
    for part in range(2):
        for a4 in range(4):
            first = (part * 4 + a4) * 8
            index = jnp.broadcast_to(cross_ref[a4 : a4 + 1, :], (8, W))
            out_ref[part, a4] = jnp.take_along_axis(total[first : first + 8], index, axis=1)


def body(vertex_matrix, vertex_site, vertex_time, vertex_spin, free_green, plus_table, cross_table):
    limit = pltpu.CompilerParams(vmem_limit_bytes=40 << 20)
    green = pl.pallas_call(
        green_kernel,
        out_shape=jax.ShapeDtypeStruct((4, W, W), BF16),
        in_specs=[ANY] * 5,
        out_specs=VMEM,
        scratch_shapes=[
            pltpu.VMEM((NV, NV), BF16),
            pltpu.VMEM((1, NV), jnp.int32),
            pltpu.VMEM((1, NV), jnp.int32),
            pltpu.VMEM((1, NV), jnp.int32),
            pltpu.VMEM((2, W), F32),
            pltpu.VMEM((4 * W, NV), BF16),
            pltpu.SemaphoreType.DMA((4 + NV // PIECE,)),
        ],
        compiler_params=pltpu.CompilerParams(vmem_limit_bytes=67043328),
        name="green",
    )(vertex_matrix, vertex_site, vertex_time, vertex_spin, free_green)
    own = lax.all_gather(green, "x", axis=0, tiled=True)
    other = lax.ppermute(own, "core", [(0, 1), (1, 0)])
    near = (lax.axis_index("x") * 2 + lax.axis_index("core")).reshape(1)
    partial = pl.pallas_call(
        pair_kernel,
        out_shape=jax.ShapeDtypeStruct((64 * 64, W), BF16),
        in_specs=[SMEM] + [VMEM] * 3,
        out_specs=VMEM,
        scratch_shapes=[
            pltpu.VMEM((NEAR, 2 * W, 2 * W), BF16),
            pltpu.VMEM((16 * W, 2 * W), BF16),
            pltpu.VMEM((4 * NEAR * PITCH, W), F32),
            pltpu.VMEM((16 * STEP, W), F32),
            pltpu.VMEM((16 * W, 16 * 4 * NEAR), F32),
            pltpu.VMEM((2 * NEAR, 16, W), F32),
            pltpu.VMEM((NEAR, 4 * W, 2 * W), F32),
            pltpu.VMEM((NEAR, 4 * W, 2 * W), F32),
            pltpu.VMEM((32, W, W), F32),
            pltpu.VMEM((32, W, W), F32),
            pltpu.VMEM((32 * PITCH, W), F32),
        ],
        compiler_params=limit,
        name="pairs",
    )(near, own, other, plus_table)
    parts = lax.all_to_all(
        partial.reshape(64, 64, W), ("y", "z_lo", "z_hi"), 0, 0, tiled=True
    )
    crossed = pl.pallas_call(
        last_kernel,
        out_shape=jax.ShapeDtypeStruct((2, 4, BROWS, W), F32),
        in_specs=[VMEM] * 2,
        out_specs=VMEM,
        compiler_params=pltpu.CompilerParams(vmem_limit_bytes=4 << 20),
        name="last",
    )(parts, cross_table)
    return jnp.swapaxes(crossed, 2, 3)


def solution(mesh):
    names = ("y", "z_lo", "z_hi", "x", "core")
    fine = Mesh(mesh.devices.reshape(8, 4, 2, 4, 2), names)
    rows = P(names)
    in_specs = (P(names, None, None), rows, rows, rows, P(), P(), P(("y", "z_lo"), None))
    out_specs = P(None, ("y", "z_lo"), None, ("z_hi", "x", "core"))
    return jax.shard_map(body, mesh=fine, in_specs=in_specs, out_specs=out_specs, check_vma=False)
```

```python
import functools
import math

import jax
import jax.numpy as jnp
from jax import lax
from jax.experimental import pallas as pl
from jax.experimental.pallas import tpu as pltpu
from jax.sharding import Mesh, PartitionSpec as P

LX = 4
NK = 16
NW = 8
W = 128
NV = 1152
NT = 1024
BROWS = 8
NEAR = 8
PIECE = 384
PITCH = W + 1
STEP = 4 * NEAR + 1
ANY = pl.BlockSpec(memory_space=pl.ANY)
VMEM = pl.BlockSpec(memory_space=pltpu.VMEM)
SMEM = pl.BlockSpec(memory_space=pltpu.SMEM)
BF16 = jnp.bfloat16
F32 = jnp.float32


def green_kernel(
    m_hbm, site_hbm, time_hbm, spin_hbm, free_hbm, out_ref,
    m_ref, site_ref, time_ref, spin_ref, free_ref, rows_ref, sems,
):
    small = [
        pltpu.make_async_copy(src, dst, sems.at[i])
        for i, (src, dst) in enumerate(
            ((site_hbm, site_ref), (time_hbm, time_ref), (spin_hbm, spin_ref), (free_hbm, free_ref))
        )
    ]
    large = [
        pltpu.make_async_copy(
            m_hbm.at[0, :, c * PIECE : (c + 1) * PIECE],
            m_ref.at[:, c * PIECE : (c + 1) * PIECE],
            sems.at[4 + c],
        )
        for c in range(NV // PIECE)
    ]
    for copy in small + large:
        copy.start()
    for copy in small:
        copy.wait()
    freq = lax.broadcasted_iota(jnp.int32, (NW, NV), 0)
    times = jnp.broadcast_to(time_ref[...], (NW, NV))
    sites = jnp.broadcast_to(site_ref[...], (NW, NV))
    spins = jnp.broadcast_to(spin_ref[...], (NW, NV))
    winding = ((2 * freq + 1) * times) & (2 * NT - 1)
    angles = winding.astype(F32) * (math.pi / NT)
    cosine, sine = jnp.cos(angles), jnp.sin(angles)
    rx, ry = sites & (LX - 1), sites >> 2
    up = (spins == 0).astype(F32)
    down = (spins == 1).astype(F32)
    for pair in range(NK // 2):
        blocks = [[], [], [], []]
        for k in (2 * pair, 2 * pair + 1):
            turns = ((k % LX) * rx + (k // LX) * ry) & 3
            odd = (turns & 1) == 1
            sign_c = jnp.where(((turns + 1) & 2) == 0, 1.0, -1.0)
            sign_s = jnp.where((turns & 2) == 0, 1.0, -1.0)
            ck = jnp.where(odd, sine, cosine) * sign_c
            sk = jnp.where(odd, cosine, sine) * sign_s
            for block, value in zip(blocks, (ck * up, sk * up, ck * down, sk * down)):
                block.append(value)
        for index, block in enumerate(blocks):
            first = index * W + pair * 2 * NW
            rows_ref[first : first + 2 * NW, :] = jnp.concatenate(block, 0).astype(BF16)
    norm_factor = 1.0 / math.sqrt(NV)
    eye = lax.broadcasted_iota(jnp.int32, (W, W), 0) == lax.broadcasted_iota(jnp.int32, (W, W), 1)
    fr, fi = free_ref[0:1, :], free_ref[1:2, :]
    col_r = jnp.sum(jnp.where(eye, fr, 0.0), axis=1, keepdims=True)
    col_i = jnp.sum(jnp.where(eye, fi, 0.0), axis=1, keepdims=True)
    pairs = [None, None]
    for c in range(NV // PIECE):
        large[c].wait()
        piece = m_ref[:, c * PIECE : (c + 1) * PIECE]
        projected = jnp.dot(rows_ref[...], piece, preferred_element_type=F32).astype(BF16)
        for s in range(2):
            mine = slice(2 * W * s, 2 * W * (s + 1))
            term = lax.dot_general(
                projected[mine],
                rows_ref[mine, c * PIECE : (c + 1) * PIECE],
                (((1,), (1,)), ((), ())),
                preferred_element_type=F32,
            )
            pairs[s] = term if c == 0 else pairs[s] + term
    for s in range(2):
        kr = pairs[s][:W, :W] + pairs[s][W:, W:]
        ki = pairs[s][W:, :W] - pairs[s][:W, W:]
        hr = col_r * kr - col_i * ki
        hi = col_r * ki + col_i * kr
        out_ref[2 * s] = (-(hr * fr - hi * fi) * norm_factor).astype(BF16)
        out_ref[2 * s + 1] = (-(hr * fi + hi * fr) * norm_factor).astype(BF16)


def tables(near, plus):
    plus_t = plus.astype(F32).T.astype(jnp.int32)
    slot = lax.broadcasted_iota(jnp.int32, (16, W), 0)
    point = lax.broadcasted_iota(jnp.int32, (16, W), 1)
    owned = (slot // 8) * 64 + near * 8 + slot % 8
    chosen = (point == owned).astype(BF16)
    plus_own = jnp.dot(chosen, plus_t.astype(F32).astype(BF16), preferred_element_type=F32)
    return plus_t, chosen, plus_own


def take_walkers(plane_ref, first, plus_t, chosen, plus_own, both_ref, lead_ref, trail_ref, col_ref):
    plus_own_i = plus_own.astype(jnp.int32)
    lane = lax.broadcasted_iota(jnp.int32, (W, W), 1)
    eye = (lax.broadcasted_iota(jnp.int32, (W, W), 0) == lane).astype(F32).astype(BF16)
    for local in range(4):
        w = first + local
        for part in range(2):
            total = None
            for s in range(2):
                value = plane_ref[local * 4 + 2 * s + part]
                both_ref[w, s * W : (s + 1) * W, part * W : (part + 1) * W] = value
                k = (w * 2 + s) * 2 + part
                lead = jnp.take_along_axis(value.astype(F32), plus_t, axis=1).astype(BF16)
                lead_ref[k * PITCH : k * PITCH + W, :] = lax.dot_general(
                    eye, lead, (((1,), (1,)), ((), ())), preferred_element_type=F32
                )
                columns = lax.dot_general(
                    chosen, value, (((1,), (1,)), ((), ())), preferred_element_type=F32
                )
                trail_ref[pl.ds(k, 16, stride=STEP), :] = jnp.take_along_axis(
                    columns, plus_own_i, axis=1
                )
                total = columns if total is None else total + columns
            col_ref[w * 2 + part] = total


def own_kernel(near_ref, own_ref, plus_ref, both_ref, pick_ref, lead_ref, trail_ref, col_ref):
    plus_t, chosen, plus_own = tables(near_ref[0], plus_ref[...])
    lane = lax.broadcasted_iota(jnp.int32, (W, W), 1)
    plus_col = plus_own.T.astype(jnp.int32)
    for b in range(16):
        hot = (plus_col[:, b : b + 1] == lane).astype(F32).astype(BF16)
        pick_ref[b * W : (b + 1) * W, 0:W] = hot
        pick_ref[b * W : (b + 1) * W, W : 2 * W] = hot
    trail_ref[...] = jnp.zeros_like(trail_ref)
    take_walkers(own_ref, 0, plus_t, chosen, plus_own, both_ref, lead_ref, trail_ref, col_ref)


def pair_kernel(
    near_ref, other_ref, plus_ref, both_own, pick_ref, lead_own, trail_own, col_own, out_ref,
    both_ref, lead_ref, trail_ref, spread_ref, col_ref, even_ref, odd_ref,
    sums_ref, straight_ref, turn_ref,
):
    def fetch(group, w, dst):
        picks = pick_ref[group * 4 * W : (group + 1) * 4 * W, :]
        dst[w] = jnp.dot(picks, both_ref[w], preferred_element_type=F32)

    both_ref[0:4] = both_own[...]
    lead_ref[0 : 16 * PITCH, :] = lead_own[...]
    trail_ref[...] = trail_own[...]
    col_ref[0:8] = col_own[...]
    for w in range(4):
        fetch(0, w, even_ref)
    plus_t, chosen, plus_own = tables(near_ref[0], plus_ref[...])
    take_walkers(other_ref, 4, plus_t, chosen, plus_own, both_ref, lead_ref, trail_ref, col_ref)
    for w in range(4, NEAR):
        fetch(0, w, even_ref)

    planes = 4 * NEAR
    from_k = lax.broadcasted_iota(jnp.int32, (planes, 16 * planes), 0)
    to_lane = lax.broadcasted_iota(jnp.int32, (planes, 16 * planes), 1)
    to_k = to_lane & (planes - 1)
    real = to_lane < 8 * planes
    repeat = jnp.where(
        real,
        jnp.where(from_k == to_k, jnp.where((to_k & 1) == 1, 1.0, -1.0), 0.0),
        jnp.where(from_k == (to_k ^ 1), -1.0, 0.0),
    ).astype(BF16)
    on = (
        (lax.broadcasted_iota(jnp.int32, (8, 16 * planes), 1) // planes) % 8
        == lax.broadcasted_iota(jnp.int32, (8, 16 * planes), 0)
    ).astype(F32)
    for b in range(16):
        turned = trail_ref[b * STEP : b * STEP + planes, :].T.astype(BF16)
        spread_ref[b * W : (b + 1) * W, :] = jnp.dot(
            turned, repeat, preferred_element_type=F32
        ) * jnp.tile(on, (16, 1))

    def exchange(t):
        left = jnp.concatenate(
            [
                spread_ref[
                    pl.ds(pl.multiple_of(b * W + t * 8, 8), 8),
                    part * 8 * planes : (part + 1) * 8 * planes,
                ]
                for part in range(2)
                for b in range(16)
            ],
            0,
        ).astype(BF16)
        right = jnp.concatenate(
            [lead_ref[pl.ds(t * 8 + j, planes, stride=PITCH), :] for j in range(8)], 0
        ).astype(BF16)
        term = jnp.dot(left, right, preferred_element_type=F32)
        for part in range(2):
            for b in range(16):
                first = (part * 16 + b) * 8
                sums_ref[2 * b + part, pl.ds(pl.multiple_of(t * 8, 8), 8), :] = term[first : first + 8]

    buffers = (even_ref, odd_ref)
    for group in range(4):
        now, later = buffers[group % 2], buffers[(group + 1) % 2]

        def direct(step, carry):
            for half in range(4):
                if group < 3 and half % 2 == 0:
                    fetch(group + 1, step * 2 + half // 2, later)
                start = pl.multiple_of(step * 32 + half * 8, 8)
                rows = pl.ds(start, 8)
                index = plus_ref[rows, :]
                for j in range(4):
                    b = group * 4 + j
                    mine = pl.ds(pl.multiple_of(j * W + start, 8), 8)
                    re = im = None
                    for v in range(NEAR):
                        row_r = col_ref[2 * v, b : b + 1, :]
                        row_i = col_ref[2 * v + 1, b : b + 1, :]
                        yr = jnp.take_along_axis(now[v, mine, 0:W], index, axis=1)
                        yi = jnp.take_along_axis(now[v, mine, W : 2 * W], index, axis=1)
                        add_r, add_i = row_r * yr - row_i * yi, row_r * yi + row_i * yr
                        re = add_r if v == 0 else re + add_r
                        im = add_i if v == 0 else im + add_i
                    straight_ref[2 * b, rows, :] = re
                    straight_ref[2 * b + 1, rows, :] = im
                if group == 0:
                    exchange(step * 4 + half)
            return carry

        lax.fori_loop(0, W // 32, direct, 0)

    def turn(step, carry):
        for j in range(4):
            b = step * 4 + j
            for part in range(2):
                turn_ref[pl.ds((part * 16 + b) * PITCH, W), :] = (straight_ref[2 * b + part] + sums_ref[2 * b + part]).T
        return carry

    lax.fori_loop(0, 4, turn, 0)

    def place(step, carry):
        for near_i, high in ((0, 0), (0, 1), (1, 0), (1, 1), (2, 0), (2, 1), (3, 0), (3, 1)):
            i = step * 4 + near_i
            for part in range(2):
                for a4 in (0, 2):
                    tiles = [
                        turn_ref[pl.ds((part * 16 + high * 8) * PITCH + i * 4 + a, 8, stride=PITCH), :]
                        for a in (a4, a4 + 1)
                    ]
                    first = pl.multiple_of((i * 2 + high) * 64 + (part * 4 + a4) * 8, 16)
                    out_ref[pl.ds(first, 16), :] = jnp.concatenate(tiles, 0).astype(BF16)
        return carry

    lax.fori_loop(0, 8, place, 0)


def last_kernel(parts_ref, cross_ref, out_ref):
    def add(step, total):
        for j in range(8):
            total = total + parts_ref[step * 8 + j].astype(F32)
        return total

    total = lax.fori_loop(0, 8, add, jnp.zeros((64, W), F32))
    for part in range(2):
        for a4 in range(4):
            first = (part * 4 + a4) * 8
            index = jnp.broadcast_to(cross_ref[a4 : a4 + 1, :], (8, W))
            out_ref[part, a4] = jnp.take_along_axis(total[first : first + 8], index, axis=1)


def body(vertex_matrix, vertex_site, vertex_time, vertex_spin, free_green, plus_table, cross_table):
    limit = pltpu.CompilerParams(vmem_limit_bytes=40 << 20)
    green = pl.pallas_call(
        green_kernel,
        out_shape=jax.ShapeDtypeStruct((4, W, W), BF16),
        in_specs=[ANY] * 5,
        out_specs=VMEM,
        scratch_shapes=[
            pltpu.VMEM((NV, NV), BF16),
            pltpu.VMEM((1, NV), jnp.int32),
            pltpu.VMEM((1, NV), jnp.int32),
            pltpu.VMEM((1, NV), jnp.int32),
            pltpu.VMEM((2, W), F32),
            pltpu.VMEM((4 * W, NV), BF16),
            pltpu.SemaphoreType.DMA((4 + NV // PIECE,)),
        ],
        compiler_params=pltpu.CompilerParams(vmem_limit_bytes=67043328),
        name="green",
    )(vertex_matrix, vertex_site, vertex_time, vertex_spin, free_green)
    own = lax.all_gather(green, "x", axis=0, tiled=True)
    other = lax.ppermute(own, "core", [(0, 1), (1, 0)])
    near = (lax.axis_index("x") * 2 + lax.axis_index("core")).reshape(1)
    half = (
        jax.ShapeDtypeStruct((4, 2 * W, 2 * W), BF16),
        jax.ShapeDtypeStruct((16 * W, 2 * W), BF16),
        jax.ShapeDtypeStruct((16 * PITCH, W), F32),
        jax.ShapeDtypeStruct((16 * STEP, W), F32),
        jax.ShapeDtypeStruct((8, 16, W), F32),
    )
    halves = pl.pallas_call(
        own_kernel,
        out_shape=half,
        in_specs=[SMEM] + [VMEM] * 2,
        out_specs=(VMEM,) * 5,
        compiler_params=pltpu.CompilerParams(vmem_limit_bytes=16 << 20),
        cost_estimate=pl.CostEstimate(flops=2 << 30, bytes_accessed=8 << 20, transcendentals=0),
        name="own",
    )(near, own, plus_table)
    partial = pl.pallas_call(
        pair_kernel,
        out_shape=jax.ShapeDtypeStruct((64 * 64, W), BF16),
        in_specs=[SMEM] + [VMEM] * 7,
        out_specs=VMEM,
        scratch_shapes=[
            pltpu.VMEM((NEAR, 2 * W, 2 * W), BF16),
            pltpu.VMEM((4 * NEAR * PITCH, W), F32),
            pltpu.VMEM((16 * STEP, W), F32),
            pltpu.VMEM((16 * W, 16 * 4 * NEAR), F32),
            pltpu.VMEM((2 * NEAR, 16, W), F32),
            pltpu.VMEM((NEAR, 4 * W, 2 * W), F32),
            pltpu.VMEM((NEAR, 4 * W, 2 * W), F32),
            pltpu.VMEM((32, W, W), F32),
            pltpu.VMEM((32, W, W), F32),
            pltpu.VMEM((32 * PITCH, W), F32),
        ],
        compiler_params=limit,
        name="pairs",
    )(near, other, plus_table, *halves)
    parts = lax.all_to_all(
        partial.reshape(64, 64, W), ("y", "z_lo", "z_hi"), 0, 0, tiled=True
    )
    crossed = pl.pallas_call(
        last_kernel,
        out_shape=jax.ShapeDtypeStruct((2, 4, BROWS, W), F32),
        in_specs=[VMEM] * 2,
        out_specs=VMEM,
        compiler_params=pltpu.CompilerParams(vmem_limit_bytes=4 << 20),
        name="last",
    )(parts, cross_table)
    return jnp.swapaxes(crossed, 2, 3)


def solution(mesh):
    names = ("y", "z_lo", "z_hi", "x", "core")
    fine = Mesh(mesh.devices.reshape(8, 4, 2, 4, 2), names)
    rows = P(names)
    in_specs = (P(names, None, None), rows, rows, rows, P(), P(), P(("y", "z_lo"), None))
    out_specs = P(None, ("y", "z_lo"), None, ("z_hi", "x", "core"))
    return jax.shard_map(body, mesh=fine, in_specs=in_specs, out_specs=out_specs, check_vma=False)
```
